512 devices in a mesh: gx: 16 (over x, z_hi), gy: 32 (over y, z_lo, core).
Axes of the slice: x: 4, y: 8, z: 8 (z_hi: 4, z_lo: 2; z = z_hi * 2 + z_lo), core: 2. Of those that a mesh axis runs over, the one named last changes fastest.
Arguments:
- object_field: float32 [2, 2, 8192, 4096], P(None, None, 'gy', 'gx'), may hold values from -5 to 5
- probe: float32 [2, 256, 256], replicated, may hold values from -6 to 6
- positions: int32 [64, 16, 2], P('gy', 'gx'), may hold values from 0 to 256, as said below
- residual: bfloat16 [64, 16, 2, 256, 256], P('gy', 'gx'), may hold values from -6 to 6
- saved_wave: bfloat16 [64, 16, 2, 256, 256], P('gy', 'gx'), may hold values from -6 to 6
Outputs:
- new_object: float32 [2, 2, 8192, 4096], P(None, None, 'gy', 'gx')
The draws below stay inside these ranges and needn't reach their ends.
Inputs may be any that keep to these rules, and one draw needn't show every extreme that they name: `positions`: row and column of each position's window corner in a frame whose anchor lies 128 cells above and to the left of its tile's first cell, so that the window stays within 128 cells of the tile; position p of a tile lies near row 128 and column 128 * (1 + p mod 2) of that frame.
All inputs are finite; a program needn't handle non-finite values.
Results may differ from the reference program's by a relative error of at most 0.0003.
Values sent between devices are 32-bit elements; how exact they have to be, the bound alone decides.
A program may use at most 64 MiB of HBM per device.

```python
import jax
import jax.numpy as jnp
from jax import lax

WIN = 256
PPD = 2
RIM = 128
TILE_ROWS = 32
TILE_COLS = 16
NR = 8192
NC = 4096


def draw_positions(key, part):
    total_rows = TILE_ROWS * PPD
    shape = (total_rows, TILE_COLS, 2)
    jitter = jax.random.randint(key, shape, -RIM, RIM + 1)
    within = jnp.arange(total_rows, dtype=jnp.int32) % PPD
    grid = jnp.stack([within // 2, within % 2], axis=-1)[:, None, :]
    anchor = jnp.clip(RIM + RIM * grid + jitter, 0, 2 * RIM)
    anchor = anchor.at[0, 0, 0].set(0)
    anchor = anchor.at[total_rows - 1, TILE_COLS - 1, 1].set(2 * RIM)
    return anchor.astype(jnp.int32)


def block_levels(own_key, extent, shards, low, top_value):
    level = 1.0
    for axis_at, blocks in shards:
        draws = jax.random.uniform(jax.random.fold_in(jax.random.fold_in(own_key, 6), axis_at), (blocks,), jnp.float32, low / len(shards), top_value / len(shards))
        level = level * jnp.repeat(jnp.exp(draws), extent[axis_at] // blocks).reshape((-1,) + (1,) * (len(extent) - 1 - axis_at))
    return level


def noise(rng, dims, deviation, reach, split=(), held_as=jnp.bfloat16):
    values = jax.random.normal(rng, dims, jnp.float32) * deviation
    if len(split) > 0:
        values = block_levels(rng, dims, split, -0.22, 0.18) * values
    return jnp.clip(values, min=-reach, max=reach).astype(held_as)


def setup_inputs(seed: int = 0) -> dict:
    key_of = jax.random.split(jax.random.key(seed), 6)
    return {
        "object_field": noise(key_of[0], (2, 2, NR, NC), 0.7, 5.0, ((2, 32), (3, 16)), jnp.float32),
        "probe": noise(key_of[1], (2, WIN, WIN), 1.0, 6.0, (), jnp.float32),
        "positions": draw_positions(jax.random.fold_in(key_of[5], 71), 0),
        "residual": noise(key_of[3], (PPD * TILE_ROWS, TILE_COLS, 2, WIN, WIN), 1.0, 6.0, ((0, 32), (1, 16))),
        "saved_wave": noise(key_of[4], (PPD * TILE_ROWS, TILE_COLS, 2, WIN, WIN), 1.0, 6.0, ((0, 32), (1, 16))),
    }


fresnel_rate = 200.0
ridge = 0.5


def kernel_conj(size):
    index = jnp.arange(size, dtype=jnp.int32)
    freq = (((index + size // 2) % size) - size // 2).astype(jnp.float32) / size
    phase = fresnel_rate * (freq[:, None] ** 2 + freq[None, :] ** 2)
    return jnp.cos(phase), jnp.sin(phase)


def reference(object_field, probe, positions, residual, saved_wave):
    rows_all = WIN * TILE_ROWS
    cols_all = WIN * TILE_COLS
    second = object_field[1, 0] + 1j * object_field[1, 1]
    padded = jnp.pad(second, RIM)
    probe_wave = probe[0] + 1j * probe[1]
    kernel_re, kernel_im = kernel_conj(WIN)
    back_kernel = kernel_re + 1j * kernel_im
    light = probe[0] * probe[0] + probe[1] * probe[1]
    initial = jnp.zeros((5, rows_all + 2 * RIM, cols_all + 2 * RIM), jnp.float32)

    def visit(carry, entry):
        row_block = entry // TILE_COLS
        column = entry % TILE_COLS
        tile_row = row_block // PPD
        top = (tile_row * WIN + positions[row_block, column, 0]).astype(jnp.int32)
        left = (column * WIN + positions[row_block, column, 1]).astype(jnp.int32)
        detector = residual[row_block, column].astype(jnp.float32)
        wave = saved_wave[row_block, column].astype(jnp.float32)
        field = jnp.fft.ifft2(detector[0] + 1j * detector[1], norm="ortho")
        patch = lax.dynamic_slice(padded, (top, left), (WIN, WIN))
        chi = jnp.conj(patch) * field
        back = jnp.fft.ifft2(back_kernel * jnp.fft.fft2(chi, norm="ortho"), norm="ortho")
        first_grad = jnp.conj(probe_wave) * back
        second_grad = jnp.conj(wave[0] + 1j * wave[1]) * field
        stacked = jnp.stack([first_grad.real, first_grad.imag, second_grad.real, second_grad.imag, light]).astype(carry.dtype)
        anchor = jnp.zeros((), jnp.int32)
        current = lax.dynamic_slice(carry, (anchor, top, left), (5, WIN, WIN))
        return lax.dynamic_update_slice(carry, current + stacked, (anchor, top, left)), None

    total_spots = TILE_ROWS * PPD * TILE_COLS
    carry, _ = lax.scan(visit, initial, jnp.arange(total_spots, dtype=jnp.int32))
    inner = carry[:, RIM:RIM + rows_all, RIM:RIM + cols_all]
    grads = inner[:4].reshape(2, 2, rows_all, cols_all)
    return object_field - grads / (inner[4] + ridge)
```

```python
import functools
import math

import jax
import jax.numpy as jnp
import numpy as np
from jax import lax
from jax.experimental import pallas as pl
from jax.experimental.pallas import tpu as pltpu
from jax.sharding import PartitionSpec as P

fresnel_rate = 200.0
ridge = 0.5
WIN = 256
RIM = 128
MESH = pl.DeviceIdType.MESH
F32 = jnp.float32
BF16 = jnp.bfloat16

O_RIGHT, O_LEFT, O_DOWN, O_UP = 0, 1, 2, 3
OC_DOWN, OC_UP = 4, 6
POS_RIGHT, POS_LEFT, POS_DOWN, POS_UP = 8, 9, 10, 11
GRAD = 12
COPIES = GRAD + 16


def split(values):
    high = values.astype(BF16)
    return high, (values - high.astype(F32)).astype(BF16)


def constant_tables():
    index = np.arange(WIN)
    angle = (np.outer(index, index) % WIN) * (2.0 * math.pi / WIN)
    freq = ((index + WIN // 2) % WIN - WIN // 2) / WIN
    phase = fresnel_rate * freq**2
    inverse = np.exp(1j * angle) / math.sqrt(WIN)
    across = inverse @ np.diag(np.exp(1j * phase)) @ np.conj(inverse)

    def pieces(table):
        parts = [table.real, table.imag]
        high = [np.asarray(t, np.float32).astype(jnp.bfloat16) for t in parts]
        low = [(t - h.astype(np.float64)).astype(np.float32).astype(jnp.bfloat16) for t, h in zip(parts, high)]
        return np.stack(high + low)

    return pieces(inverse), pieces(across)


def dot(a, b):
    return jnp.dot(a, b, preferred_element_type=F32)


def kernel(
    rows,
    cols,
    pos_ref,
    obj_hbm,
    probe_hbm,
    res_hbm,
    sav_hbm,
    tab_hbm,
    atab_hbm,
    out_hbm,
    obj,
    probe,
    res,
    sav,
    tab,
    atab,
    ext,
    posx,
    posall,
    frame,
    from_up,
    from_down,
    from_left,
    from_right,
    side,
    left_tab,
    right_tab,
    left_a,
    right_a,
    fields,
    pair,
    big,
    gbuf,
    pbuf,
    lsq,
    light,
    obuf,
    send_sem,
    recv_sem,
    load_sem,
):
    gx = lax.axis_index("gx")
    gy = lax.axis_index("gy")
    right = {"gx": lax.rem(gx + 1, cols)}
    left = {"gx": lax.rem(gx + cols - 1, cols)}
    down = {"gy": lax.rem(gy + 1, rows)}
    up = {"gy": lax.rem(gy + rows - 1, rows)}

    loads = []

    def load(source, target):
        copy = pltpu.make_async_copy(source, target, load_sem.at[len(loads)])
        copy.start()
        loads.append(copy)

    load(res_hbm, res.at[:, 0:512])
    load(res_hbm, res.at[:, 512:1024])
    load(tab_hbm, tab)
    load(sav_hbm, sav)
    load(probe_hbm, probe)
    load(atab_hbm, atab)
    load(obj_hbm.at[1], ext.at[:, RIM : 3 * RIM, RIM : 3 * RIM])
    load(obj_hbm, obj)

    barrier = pltpu.get_barrier_semaphore()
    for neighbour in (left, right, up, down):
        pl.semaphore_signal(barrier, inc=1, device_id=neighbour, device_id_type=MESH)
    pl.semaphore_wait(barrier, 4)

    copies = {}

    def send(source, target, number, to):
        copy = pltpu.make_async_remote_copy(
            src_ref=source,
            dst_ref=target,
            send_sem=send_sem.at[number],
            recv_sem=recv_sem.at[number],
            device_id=to,
            device_id_type=MESH,
        )
        copy.start()
        copies[number] = copy

    def arrived(*numbers):
        for number in numbers:
            copies[number].wait_recv()

    send(obj_hbm.at[1, :, :, RIM:], ext.at[:, RIM : 3 * RIM, 0:RIM], O_RIGHT, right)
    send(obj_hbm.at[1, :, :, 0:RIM], ext.at[:, RIM : 3 * RIM, 3 * RIM :], O_LEFT, left)
    for number in range(2):
        for axis in range(2):
            value = pos_ref[number, axis].astype(F32)
            posx[1, 2 * number + axis : 2 * number + axis + 1, :] = jnp.full((1, 128), value, F32)
    posx[1, 4:8, :] = jnp.zeros((4, 128), F32)
    send(obj_hbm.at[1, :, RIM:, :], ext.at[:, 0:RIM, RIM : 3 * RIM], O_DOWN, down)
    send(obj_hbm.at[1, :, 0:RIM, :], ext.at[:, 3 * RIM :, RIM : 3 * RIM], O_UP, up)
    send(posx.at[1], posx.at[0], POS_RIGHT, right)
    send(posx.at[1], posx.at[2], POS_LEFT, left)

    row_index = lax.broadcasted_iota(jnp.int32, (WIN, WIN), 0)
    col_index = lax.broadcasted_iota(jnp.int32, (WIN, WIN), 1)

    def turn(shift):
        offset = row_index - col_index
        hit = (offset == shift) | (offset == shift - WIN)
        return jnp.where(hit, 1.0, 0.0).astype(BF16)

    def turn_columns(shift):
        offset = col_index - row_index
        hit = (offset == shift) | (offset == shift - WIN)
        return jnp.where(hit, 1.0, 0.0).astype(BF16)

    def place(target, field, row, col):
        for a in range(2):
            low = row_index >= row if a == 0 else row_index < row
            for b in range(2):
                hit = low & (col_index >= col if b == 0 else col_index < col)
                spot = (slice(a * WIN, (a + 1) * WIN), slice(b * WIN, (b + 1) * WIN))
                target[spot] = target[spot] + jnp.where(hit, field, 0.0)

    frame[...] = jnp.zeros_like(frame)
    for copy in loads:
        copy.wait()

    def first(number, carry):
        row = pos_ref[number, 0]
        col = pos_ref[number, 1]
        rows_turned = turn(row)
        cols_turned = turn_columns(col)
        for half in range(2):
            cos = dot(rows_turned, tab[2 * half])
            sin = dot(rows_turned, tab[2 * half + 1])
            at = 512 * half
            left_tab[0:256, at : at + 256] = cos.astype(BF16)
            left_tab[0:256, at + 256 : at + 512] = (-sin).astype(BF16)
            left_tab[256:512, at : at + 256] = sin.astype(BF16)
            left_tab[256:512, at + 256 : at + 512] = cos.astype(BF16)
            cos = dot(tab[2 * half], cols_turned)
            sin = dot(tab[2 * half + 1], cols_turned)
            for at in (0, 512) if half == 0 else (1024,):
                right_tab[at : at + 256, 0:256] = cos.astype(BF16)
                right_tab[at : at + 256, 256:512] = sin.astype(BF16)
                right_tab[at + 256 : at + 512, 0:256] = (-sin).astype(BF16)
                right_tab[at + 256 : at + 512, 256:512] = cos.astype(BF16)
        half_way = dot(left_tab[...], res[number])
        high, low = split(half_way)
        for part in range(2):
            span = slice(256 * part, 256 * part + 256)
            for at, piece in ((0, high), (512, low), (1024, high)):
                pair[0:256, at + 256 * part : at + 256 * part + 256] = piece[span]
        field = dot(pair[0:256, :], right_tab[...])
        gbuf[number] = field
        field_re = field[:, 0:256]
        field_im = field[:, 256:512]
        wave_re = dot(dot(rows_turned, sav[number, 0]).astype(BF16), cols_turned)
        wave_im = dot(dot(rows_turned, sav[number, 1]).astype(BF16), cols_turned)
        place(frame.at[0, 0], wave_re * field_re + wave_im * field_im, row, col)
        place(frame.at[0, 1], wave_re * field_im - wave_im * field_re, row, col)
        for part in range(2):
            high, low = split(probe[part])
            high = dot(dot(rows_turned, high).astype(BF16), cols_turned)
            low = dot(dot(rows_turned, low).astype(BF16), cols_turned)
            pbuf[number, part] = high + low
        return carry

    lax.fori_loop(0, 2, first, 0)

    for half in range(2):
        real = atab[2 * half]
        imag = atab[2 * half + 1]
        for at in (0, 512) if half == 0 else (1024,):
            left_a[0:256, at : at + 256] = real
            left_a[0:256, at + 256 : at + 512] = -imag
            left_a[256:512, at : at + 256] = imag
            left_a[256:512, at + 256 : at + 512] = real
            right_a[at : at + 256, 0:256] = real
            right_a[at : at + 256, 256:512] = imag
            right_a[at + 256 : at + 512, 0:256] = -imag
            right_a[at + 256 : at + 512, 256:512] = real
    high, low = split(probe[0] * probe[0] + probe[1] * probe[1])
    lsq[0] = high
    lsq[1] = low

    def send_rows(group):
        base = GRAD + 8 * group
        for v, at in ((0, 0), (1, 3 * RIM)):
            send(
                frame.at[group, :, 3 * RIM :, at : at + RIM],
                from_up.at[group, :, :, at : at + RIM],
                base + v,
                down,
            )
            send(
                frame.at[group, :, 0:RIM, at : at + RIM],
                from_down.at[group, :, :, at : at + RIM],
                base + 2 + v,
                up,
            )
        centre = slice(RIM, 3 * RIM)
        send(frame.at[group, :, 3 * RIM :, centre], from_up.at[group, :, :, centre], base + 4, down)
        send(frame.at[group, :, 0:RIM, centre], from_down.at[group, :, :, centre], base + 5, up)

    def drop_rows(group, spans):
        @pl.when(gy == 0)
        def _():
            for span in spans:
                from_up[group, :, :, span] = jnp.zeros((2, RIM, span.stop - span.start), F32)

        @pl.when(gy == rows - 1)
        def _():
            for span in spans:
                from_down[group, :, :, span] = jnp.zeros((2, RIM, span.stop - span.start), F32)

    def send_sides(group):
        base = GRAD + 8 * group
        arrived(base, base + 1, base + 2, base + 3)
        drop_rows(group, (slice(0, RIM), slice(3 * RIM, 4 * RIM)))
        for which, at in ((0, 3 * RIM), (1, 0)):
            span = slice(at, at + RIM)
            side[group, which, :, 0:RIM] = frame[group, :, RIM : 2 * RIM, span] + from_up[group, :, :, span]
            side[group, which, :, RIM:] = frame[group, :, 2 * RIM : 3 * RIM, span] + from_down[group, :, :, span]
        send(side.at[group, 0], from_left.at[group], base + 6, right)
        send(side.at[group, 1], from_right.at[group], base + 7, left)

    def finish(group):
        base = GRAD + 8 * group
        arrived(base + 4, base + 5)
        drop_rows(group, (slice(RIM, 3 * RIM),))
        arrived(base + 6, base + 7)

        @pl.when(gx == 0)
        def _():
            from_left[group] = jnp.zeros((2, WIN, RIM), F32)

        @pl.when(gx == cols - 1)
        def _():
            from_right[group] = jnp.zeros((2, WIN, RIM), F32)

        for part in range(2):
            for h, vertical in ((0, from_up), (1, from_down)):
                for v, horizontal in ((0, from_left), (1, from_right)):
                    tall = slice(h * RIM, h * RIM + RIM)
                    wide = slice(v * RIM, v * RIM + RIM)
                    total = (
                        frame[group, part, RIM + h * RIM : 2 * RIM + h * RIM, RIM + v * RIM : 2 * RIM + v * RIM]
                        + vertical[group, part, :, RIM + v * RIM : 2 * RIM + v * RIM]
                        + horizontal[group, part, tall, :]
                    )
                    obuf[1 - group, part, tall, wide] = obj[1 - group, part, tall, wide] - total / light[tall, wide]
        copy = pltpu.make_async_copy(obuf.at[1 - group], out_hbm.at[1 - group], load_sem.at[8 + group])
        copy.start()
        return copy

    arrived(O_RIGHT, O_LEFT)
    for v, at in ((0, 0), (1, 3 * RIM)):
        span = slice(at, at + RIM)
        send(ext.at[:, 2 * RIM : 3 * RIM, span], ext.at[:, 0:RIM, span], OC_DOWN + v, down)
        send(ext.at[:, RIM : 2 * RIM, span], ext.at[:, 3 * RIM :, span], OC_UP + v, up)
    arrived(POS_RIGHT, POS_LEFT)
    posall[1] = posx[...]
    send(posx, posall.at[0], POS_DOWN, down)
    send(posx, posall.at[2], POS_UP, up)
    send_rows(0)

    light[...] = jnp.full((WIN, WIN), ridge, F32)
    arrived(POS_DOWN, POS_UP)
    offset = (row_index - col_index).astype(F32)

    def lit(number, carry):
        dy = number // 3 - 1
        dx = number % 3 - 1
        inside = (gy + dy >= 0) & (gy + dy < rows) & (gx + dx >= 0) & (gx + dx < cols)
        weight = jnp.where(inside, 1.0, 0.0)
        spots = posall[number // 3, number % 3]
        total = light[...]
        for spot in range(2):
            row = spots[2 * spot : 2 * spot + 1, :] + (dy * WIN - RIM).astype(F32)
            col = spots[2 * spot + 1 : 2 * spot + 2, :] + (dx * WIN - RIM).astype(F32)
            row = jnp.concatenate([row, row], axis=1)
            col = jnp.concatenate([col, col], axis=1)
            by_rows = jnp.where(offset == row, weight, 0.0).astype(BF16)
            by_cols = jnp.where(-offset == col, 1.0, 0.0).astype(BF16)
            for part in range(2):
                total = total + dot(by_rows, dot(lsq[part], by_cols).astype(BF16))
        light[...] = total
        return carry

    lax.fori_loop(0, 9, lit, 0)

    arrived(O_DOWN, O_UP, OC_DOWN, OC_DOWN + 1, OC_UP, OC_UP + 1)

    first_row = jnp.where(gy == 0, RIM, 0)
    last_row = jnp.where(gy == rows - 1, 3 * RIM, 4 * RIM)
    first_col = jnp.where(gx == 0, RIM, 0)
    last_col = jnp.where(gx == cols - 1, 3 * RIM, 4 * RIM)

    for number in range(2):
        row = pos_ref[number, 0]
        col = pos_ref[number, 1]
        upper = row_index >= row
        leftmost = col_index >= col
        at_row = jnp.where(upper, row_index, row_index + WIN)
        at_col = jnp.where(leftmost, col_index, col_index + WIN)
        inside = (at_row >= first_row) & (at_row < last_row) & (at_col >= first_col) & (at_col < last_col)
        patch = []
        for part in range(2):
            top = jnp.where(leftmost, ext[part, 0:256, 0:256], ext[part, 0:256, 256:512])
            bottom = jnp.where(leftmost, ext[part, 256:512, 0:256], ext[part, 256:512, 256:512])
            patch.append(jnp.where(inside, jnp.where(upper, top, bottom), 0.0))
        field_re = gbuf[number, :, 0:256]
        field_im = gbuf[number, :, 256:512]
        chi = (
            patch[0] * field_re + patch[1] * field_im,
            patch[0] * field_im - patch[1] * field_re,
        )
        for part in range(2):
            high, low = split(chi[part])
            for at, piece in ((0, high), (512, low), (1024, high)):
                fields[at + 256 * part : at + 256 * part + 256, 256 * number : 256 * number + 256] = piece
    big[...] = dot(left_a[...], fields[...])
    for number in range(2):
        for part in range(2):
            high, low = split(big[256 * part : 256 * part + 256, 256 * number : 256 * number + 256])
            for at, piece in ((0, high), (512, low), (1024, high)):
                pair[256 * number : 256 * number + 256, at + 256 * part : at + 256 * part + 256] = piece
    big[...] = dot(pair[...], right_a[...])

    def second(number, carry):
        row = pos_ref[number, 0]
        col = pos_ref[number, 1]
        span = pl.ds(pl.multiple_of(number * 256, 256), 256)
        back_re = big[span, 0:256]
        back_im = big[span, 256:512]
        probe_re = pbuf[number, 0]
        probe_im = pbuf[number, 1]
        place(frame.at[1, 0], probe_re * back_re + probe_im * back_im, row, col)
        place(frame.at[1, 1], probe_re * back_im - probe_im * back_re, row, col)
        return carry

    lax.fori_loop(0, 2, second, 0)
    send_sides(0)
    send_rows(1)
    send_sides(1)
    stores = [finish(0), finish(1)]
    for copy in stores:
        copy.wait()
    for number in range(COPIES):
        copies[number].wait_send()


def solution(mesh):
    rows, cols = mesh.shape["gy"], mesh.shape["gx"]
    tab, atab = constant_tables()

    def step(object_field, probe, positions, residual, saved_wave):
        anywhere = pl.BlockSpec(memory_space=pl.ANY)
        vmem = pltpu.VMEM
        return pl.pallas_call(
            functools.partial(kernel, rows, cols),
            name="adjoint",
            out_shape=jax.ShapeDtypeStruct((2, 2, WIN, WIN), F32),
            in_specs=[pl.BlockSpec(memory_space=pltpu.SMEM)] + [anywhere] * 6,
            out_specs=anywhere,
            scratch_shapes=[
                vmem((2, 2, WIN, WIN), F32),
                vmem((2, WIN, WIN), F32),
                vmem((2, 1024, WIN), BF16),
                vmem((2, 2, WIN, WIN), BF16),
                vmem((4, WIN, WIN), BF16),
                vmem((4, WIN, WIN), BF16),
                vmem((2, 512, 512), F32),
                vmem((3, 8, 128), F32),
                vmem((3, 3, 8, 128), F32),
                vmem((2, 2, 512, 512), F32),
                vmem((2, 2, RIM, 512), F32),
                vmem((2, 2, RIM, 512), F32),
                vmem((2, 2, WIN, RIM), F32),
                vmem((2, 2, WIN, RIM), F32),
                vmem((2, 2, 2, WIN, RIM), F32),
                vmem((512, 1024), BF16),
                vmem((1536, 512), BF16),
                vmem((512, 1536), BF16),
                vmem((1536, 512), BF16),
                vmem((1536, 512), BF16),
                vmem((512, 1536), BF16),
                vmem((512, 512), F32),
                vmem((2, WIN, 512), F32),
                vmem((2, 2, WIN, WIN), F32),
                vmem((2, WIN, WIN), BF16),
                vmem((WIN, WIN), F32),
                vmem((2, 2, WIN, WIN), F32),
                pltpu.SemaphoreType.DMA((COPIES,)),
                pltpu.SemaphoreType.DMA((COPIES,)),
                pltpu.SemaphoreType.DMA((10,)),
            ],
            compiler_params=pltpu.CompilerParams(
                collective_id=0, has_side_effects=True, vmem_limit_bytes=56 * 1024 * 1024
            ),
        )(
            positions.reshape(2, 2),
            object_field,
            probe,
            residual.reshape(2, 512, WIN),
            saved_wave.reshape(2, 2, WIN, WIN),
            jnp.asarray(tab),
            jnp.asarray(atab),
        )

    placed = (
        P(None, None, "gy", "gx"),
        P(),
        P("gy", "gx", None),
        P("gy", "gx", None, None, None),
        P("gy", "gx", None, None, None),
    )
    return jax.shard_map(
        step, mesh=mesh, in_specs=placed, out_specs=P(None, None, "gy", "gx"), check_vma=False
    )
```

```python
import functools
import math

import jax
import jax.numpy as jnp
import numpy as np
from jax import lax
from jax.experimental import pallas as pl
from jax.experimental.pallas import tpu as pltpu
from jax.sharding import PartitionSpec as P

fresnel_rate = 200.0
ridge = 0.5
WIN = 256
RIM = 128
MESH = pl.DeviceIdType.MESH
F32 = jnp.float32
BF16 = jnp.bfloat16

O_RIGHT, O_LEFT = 0, 1
C_INNER, C_STRAIGHT, C_DIAGONAL, C_EDGE = 2, 3, 4, 5
H_INNER, H_STRAIGHT, H_DIAGONAL = 6, 8, 9
POS_RIGHT, POS_LEFT, POS_INNER, POS_OUTER = 10, 11, 12, 13
GRAD = 14
COPIES = GRAD + 12


def split(values):
    high = values.astype(BF16)
    return high, (values - high.astype(F32)).astype(BF16)


def constant_tables():
    index = np.arange(WIN)
    angle = (np.outer(index, index) % WIN) * (2.0 * math.pi / WIN)
    freq = ((index + WIN // 2) % WIN - WIN // 2) / WIN
    phase = fresnel_rate * freq**2
    inverse = np.exp(1j * angle) / math.sqrt(WIN)
    across = inverse @ np.diag(np.exp(1j * phase)) @ np.conj(inverse)

    def pieces(table):
        parts = [table.real, table.imag]
        high = [np.asarray(t, np.float32).astype(jnp.bfloat16) for t in parts]
        low = [(t - h.astype(np.float64)).astype(np.float32).astype(jnp.bfloat16) for t, h in zip(parts, high)]
        return np.stack(high + low)

    return pieces(inverse), pieces(across)


def dot(a, b):
    return jnp.dot(a, b, preferred_element_type=F32)


def kernel(
    rows,
    cols,
    pos_ref,
    obj_hbm,
    probe_hbm,
    res_hbm,
    sav_hbm,
    tab_hbm,
    atab_hbm,
    out_hbm,
    obj,
    probe,
    res,
    sav,
    tab,
    atab,
    ext,
    posx,
    posall,
    frame,
    within,
    straight,
    slanted,
    edge,
    from_left,
    from_right,
    side,
    left_tab,
    right_tab,
    left_a,
    right_a,
    fields,
    pair,
    big,
    gbuf,
    pbuf,
    lsq,
    light,
    obuf,
    send_sem,
    recv_sem,
    load_sem,
):
    gx = lax.axis_index("gx")
    gy = lax.axis_index("gy")
    core = gy % 2
    parity = (gy // 2) % 2
    out_row = gy - 1 + 2 * core
    side_col = gx - 1 + 2 * parity
    has_left, has_right = gx > 0, gx < cols - 1
    has_outer = (out_row >= 0) & (out_row < rows)
    has_side = (side_col >= 0) & (side_col < cols)
    has_diagonal = has_outer & has_side
    lone = has_outer & jnp.logical_not(has_side)
    facing = has_outer & (((gx == 0) & (parity == 1)) | ((gx == cols - 1) & (parity == 0)))
    right = {"gx": lax.rem(gx + 1, cols)}
    left = {"gx": lax.rem(gx + cols - 1, cols)}
    inner = {"gy": gy + 1 - 2 * core}
    outer = {"gy": lax.rem(out_row + rows, rows)}
    diagonal = {"gx": lax.rem(side_col + cols, cols), "gy": lax.rem(out_row + rows, rows)}

    def cut(start, size=RIM):
        return pl.ds(pl.multiple_of(start, RIM), size)

    loads = []

    def load(source, target):
        copy = pltpu.make_async_copy(source, target, load_sem.at[len(loads)])
        copy.start()
        loads.append(copy)

    load(res_hbm, res.at[:, 0:512])
    load(res_hbm, res.at[:, 512:1024])
    load(tab_hbm, tab)
    load(sav_hbm, sav)
    load(probe_hbm, probe)
    load(atab_hbm, atab)
    load(obj_hbm.at[1], ext.at[:, RIM : 3 * RIM, RIM : 3 * RIM])
    load(obj_hbm, obj)

    frame[...] = jnp.zeros_like(frame)

    @pl.when(gx == 0)
    def _():
        ext[:, RIM : 3 * RIM, 0:RIM] = jnp.zeros((2, WIN, RIM), F32)

    @pl.when(gx == cols - 1)
    def _():
        ext[:, RIM : 3 * RIM, 3 * RIM :] = jnp.zeros((2, WIN, RIM), F32)

    barrier = pltpu.get_barrier_semaphore()
    greeted = 1
    pl.semaphore_signal(barrier, inc=1, device_id=inner, device_id_type=MESH)
    for there, who in ((has_left, left), (has_right, right), (has_outer, outer), (has_diagonal, diagonal)):
        @pl.when(there)
        def _():
            pl.semaphore_signal(barrier, inc=1, device_id=who, device_id_type=MESH)

        greeted = greeted + there.astype(jnp.int32)
    pl.semaphore_wait(barrier, greeted)

    copies = {}

    def send(source, target, number, to, there=None, comes=None):
        copy = pltpu.make_async_remote_copy(
            src_ref=source,
            dst_ref=target,
            send_sem=send_sem.at[number],
            recv_sem=recv_sem.at[number],
            device_id=to,
            device_id_type=MESH,
        )
        comes = there if comes is None else comes
        copies[number] = (copy, there, comes)
        if there is None:
            copy.start()
        else:
            pl.when(there)(copy.start)

    def arrived(*numbers):
        for number in numbers:
            copy, _, comes = copies[number]
            if comes is None:
                copy.wait_recv()
            else:
                pl.when(comes)(copy.wait_recv)

    send(obj_hbm.at[1, :, :, RIM:], ext.at[:, RIM : 3 * RIM, 0:RIM], O_RIGHT, right, has_right, has_left)
    send(obj_hbm.at[1, :, :, 0:RIM], ext.at[:, RIM : 3 * RIM, 3 * RIM :], O_LEFT, left, has_left, has_right)
    near = 128 * parity
    halo = 384 * parity
    over = WIN * (1 - 2 * parity)
    below = RIM * core
    above = RIM - RIM * core
    outside = 3 * RIM * (1 - core)
    inside_row = 3 * RIM * core
    send(obj_hbm.at[1, :, cut(below), cut(near)], ext.at[:, cut(outside), cut(RIM + near)], C_STRAIGHT, outer, has_outer)
    send(
        obj_hbm.at[1, :, cut(below), cut(near)],
        ext.at[:, cut(outside), cut(RIM + near + over)],
        C_DIAGONAL,
        diagonal,
        has_diagonal,
    )
    send(
        obj_hbm.at[1, :, cut(below), cut(RIM - near)],
        ext.at[:, cut(outside), cut(WIN - near)],
        C_EDGE,
        outer,
        facing,
        lone,
    )
    send(obj_hbm.at[1, :, cut(above), :], ext.at[:, cut(inside_row), RIM : 3 * RIM], C_INNER, inner)
    for number in range(2):
        for axis in range(2):
            value = pos_ref[number, axis].astype(F32)
            posx[1, 2 * number + axis : 2 * number + axis + 1, :] = jnp.full((1, 128), value, F32)
    posx[1, 4:8, :] = jnp.zeros((4, 128), F32)
    send(posx.at[1], posx.at[0], POS_RIGHT, right, has_right, has_left)
    send(posx.at[1], posx.at[2], POS_LEFT, left, has_left, has_right)

    row_index = lax.broadcasted_iota(jnp.int32, (WIN, WIN), 0)
    col_index = lax.broadcasted_iota(jnp.int32, (WIN, WIN), 1)

    def turn(shift):
        offset = row_index - col_index
        hit = (offset == shift) | (offset == shift - WIN)
        return jnp.where(hit, 1.0, 0.0).astype(BF16)

    def turn_columns(shift):
        offset = col_index - row_index
        hit = (offset == shift) | (offset == shift - WIN)
        return jnp.where(hit, 1.0, 0.0).astype(BF16)

    def place(target, field, row, col):
        for a in range(2):
            low = row_index >= row if a == 0 else row_index < row
            for b in range(2):
                hit = low & (col_index >= col if b == 0 else col_index < col)
                spot = (slice(a * WIN, (a + 1) * WIN), slice(b * WIN, (b + 1) * WIN))
                target[spot] = target[spot] + jnp.where(hit, field, 0.0)

    for copy in loads:
        copy.wait()

    def first(number, carry):
        row = pos_ref[number, 0]
        col = pos_ref[number, 1]
        rows_turned = turn(row)
        cols_turned = turn_columns(col)
        for half in range(2):
            cos = dot(rows_turned, tab[2 * half])
            sin = dot(rows_turned, tab[2 * half + 1])
            at = 512 * half
            left_tab[0:256, at : at + 256] = cos.astype(BF16)
            left_tab[0:256, at + 256 : at + 512] = (-sin).astype(BF16)
            left_tab[256:512, at : at + 256] = sin.astype(BF16)
            left_tab[256:512, at + 256 : at + 512] = cos.astype(BF16)
            cos = dot(tab[2 * half], cols_turned)
            sin = dot(tab[2 * half + 1], cols_turned)
            for at in (0, 512) if half == 0 else (1024,):
                right_tab[at : at + 256, 0:256] = cos.astype(BF16)
                right_tab[at : at + 256, 256:512] = sin.astype(BF16)
                right_tab[at + 256 : at + 512, 0:256] = (-sin).astype(BF16)
                right_tab[at + 256 : at + 512, 256:512] = cos.astype(BF16)
        half_way = dot(left_tab[...], res[number])
        high, low = split(half_way)
        for part in range(2):
            span = slice(256 * part, 256 * part + 256)
            for at, piece in ((0, high), (512, low), (1024, high)):
                pair[0:256, at + 256 * part : at + 256 * part + 256] = piece[span]
        field = dot(pair[0:256, :], right_tab[...])
        gbuf[number] = field
        field_re = field[:, 0:256]
        field_im = field[:, 256:512]
        wave_re = dot(dot(rows_turned, sav[number, 0]).astype(BF16), cols_turned)
        wave_im = dot(dot(rows_turned, sav[number, 1]).astype(BF16), cols_turned)
        place(frame.at[0, 0], wave_re * field_re + wave_im * field_im, row, col)
        place(frame.at[0, 1], wave_re * field_im - wave_im * field_re, row, col)
        for part in range(2):
            high, low = split(probe[part])
            high = dot(dot(rows_turned, high).astype(BF16), cols_turned)
            low = dot(dot(rows_turned, low).astype(BF16), cols_turned)
            pbuf[number, part] = high + low
        return carry

    lax.fori_loop(0, 2, first, 0)

    for half in range(2):
        real = atab[2 * half]
        imag = atab[2 * half + 1]
        for at in (0, 512) if half == 0 else (1024,):
            left_a[0:256, at : at + 256] = real
            left_a[0:256, at + 256 : at + 512] = -imag
            left_a[256:512, at : at + 256] = imag
            left_a[256:512, at + 256 : at + 512] = real
            right_a[at : at + 256, 0:256] = real
            right_a[at : at + 256, 256:512] = imag
            right_a[at + 256 : at + 512, 0:256] = -imag
            right_a[at + 256 : at + 512, 256:512] = real
    high, low = split(probe[0] * probe[0] + probe[1] * probe[1])
    lsq[0] = high
    lsq[1] = low

    def send_rows(group):
        base = GRAD + 6 * group
        send(frame.at[group, :, cut(3 * RIM * core), cut(WIN - WIN * parity, WIN)], straight.at[group], base + 1, outer, has_outer)
        send(frame.at[group, :, cut(3 * RIM * core), cut(WIN * parity, WIN)], slanted.at[group], base + 2, diagonal, has_diagonal)
        send(frame.at[group, :, cut(3 * RIM * core), cut(RIM + near)], edge.at[group], base + 3, outer, lone, facing)
        send(frame.at[group, :, cut(3 * RIM - 3 * RIM * core), :], within.at[group], base, inner)

    def send_sides(group):
        base = GRAD + 6 * group
        arrived(base, base + 1, base + 2, base + 3)
        for part in range(2):
            spot = (group, part, cut(WIN - RIM * core), slice(None))
            frame[spot] = frame[spot] + within[group, part]
            spot = (group, part, cut(RIM + RIM * core), cut(WIN * parity, WIN))
            for there, piece in ((has_outer, straight), (has_diagonal, slanted)):
                @pl.when(there)
                def _():
                    frame[spot] = frame[spot] + piece[group, part]

            @pl.when(facing)
            def _():
                spot = (group, part, cut(RIM + RIM * core), cut(WIN - near))
                frame[spot] = frame[spot] + edge[group, part]

        middle = slice(RIM, 3 * RIM)
        side[group, 0] = frame[group, :, middle, 3 * RIM :]
        side[group, 1] = frame[group, :, middle, 0:RIM]
        send(side.at[group, 0], from_left.at[group], base + 4, right, has_right, has_left)
        send(side.at[group, 1], from_right.at[group], base + 5, left, has_left, has_right)

    def finish(group):
        base = GRAD + 6 * group

        @pl.when(gx == 0)
        def _():
            from_left[group] = jnp.zeros((2, WIN, RIM), F32)

        @pl.when(gx == cols - 1)
        def _():
            from_right[group] = jnp.zeros((2, WIN, RIM), F32)

        arrived(base + 4, base + 5)
        for part in range(2):
            for v, horizontal in ((0, from_left), (1, from_right)):
                wide = slice(v * RIM, v * RIM + RIM)
                total = (
                    frame[group, part, RIM : 3 * RIM, RIM + v * RIM : 2 * RIM + v * RIM]
                    + horizontal[group, part]
                )
                obuf[1 - group, part, :, wide] = obj[1 - group, part, :, wide] - total / light[:, wide]
        copy = pltpu.make_async_copy(obuf.at[1 - group], out_hbm.at[1 - group], load_sem.at[8 + group])
        copy.start()
        return copy

    arrived(O_RIGHT, O_LEFT)
    rows_out, rows_in = cut(RIM + below), cut(RIM + above)
    send(ext.at[:, rows_out, cut(halo)], ext.at[:, cut(outside), cut(halo)], H_STRAIGHT, outer, has_outer)
    send(ext.at[:, rows_out, cut(halo)], ext.at[:, cut(outside), cut(halo + over)], H_DIAGONAL, diagonal, has_diagonal)
    for v, span in ((0, slice(0, RIM)), (1, slice(3 * RIM, 4 * RIM))):
        send(ext.at[:, rows_in, span], ext.at[:, cut(inside_row), span], H_INNER + v, inner)
    arrived(POS_RIGHT, POS_LEFT)
    posall[1] = posx[...]
    send(posx, posall.at[2 - 2 * (1 - core)], POS_INNER, inner)
    send(posx, posall.at[2 - 2 * core], POS_OUTER, outer, has_outer)
    send_rows(0)

    light[...] = jnp.full((WIN, WIN), ridge, F32)
    arrived(POS_INNER, POS_OUTER)
    offset = (row_index - col_index).astype(F32)

    def lit(number, carry):
        dy = number // 3 - 1
        dx = number % 3 - 1
        inside = (gy + dy >= 0) & (gy + dy < rows) & (gx + dx >= 0) & (gx + dx < cols)
        weight = jnp.where(inside, 1.0, 0.0)
        spots = posall[number // 3, number % 3]
        total = light[...]
        for spot in range(2):
            row = spots[2 * spot : 2 * spot + 1, :] + (dy * WIN - RIM).astype(F32)
            col = spots[2 * spot + 1 : 2 * spot + 2, :] + (dx * WIN - RIM).astype(F32)
            row = jnp.concatenate([row, row], axis=1)
            col = jnp.concatenate([col, col], axis=1)
            by_rows = jnp.where(offset == row, weight, 0.0).astype(BF16)
            by_cols = jnp.where(-offset == col, 1.0, 0.0).astype(BF16)
            for part in range(2):
                total = total + dot(by_rows, dot(lsq[part], by_cols).astype(BF16))
        light[...] = total
        return carry

    lax.fori_loop(0, 9, lit, 0)

    arrived(C_INNER, C_STRAIGHT, C_DIAGONAL, C_EDGE, H_INNER, H_INNER + 1, H_STRAIGHT, H_DIAGONAL)

    first_row = jnp.where(gy == 0, RIM, 0)
    last_row = jnp.where(gy == rows - 1, 3 * RIM, 4 * RIM)
    first_col = jnp.where(gx == 0, RIM, 0)
    last_col = jnp.where(gx == cols - 1, 3 * RIM, 4 * RIM)

    for number in range(2):
        row = pos_ref[number, 0]
        col = pos_ref[number, 1]
        upper = row_index >= row
        leftmost = col_index >= col
        at_row = jnp.where(upper, row_index, row_index + WIN)
        at_col = jnp.where(leftmost, col_index, col_index + WIN)
        inside = (at_row >= first_row) & (at_row < last_row) & (at_col >= first_col) & (at_col < last_col)
        patch = []
        for part in range(2):
            top = jnp.where(leftmost, ext[part, 0:256, 0:256], ext[part, 0:256, 256:512])
            bottom = jnp.where(leftmost, ext[part, 256:512, 0:256], ext[part, 256:512, 256:512])
            patch.append(jnp.where(inside, jnp.where(upper, top, bottom), 0.0))
        field_re = gbuf[number, :, 0:256]
        field_im = gbuf[number, :, 256:512]
        chi = (
            patch[0] * field_re + patch[1] * field_im,
            patch[0] * field_im - patch[1] * field_re,
        )
        for part in range(2):
            high, low = split(chi[part])
            for at, piece in ((0, high), (512, low), (1024, high)):
                fields[at + 256 * part : at + 256 * part + 256, 256 * number : 256 * number + 256] = piece
    big[...] = dot(left_a[...], fields[...])
    for number in range(2):
        for part in range(2):
            high, low = split(big[256 * part : 256 * part + 256, 256 * number : 256 * number + 256])
            for at, piece in ((0, high), (512, low), (1024, high)):
                pair[256 * number : 256 * number + 256, at + 256 * part : at + 256 * part + 256] = piece
    big[...] = dot(pair[...], right_a[...])

    def second(number, carry):
        row = pos_ref[number, 0]
        col = pos_ref[number, 1]
        span = pl.ds(pl.multiple_of(number * 256, 256), 256)
        back_re = big[span, 0:256]
        back_im = big[span, 256:512]
        probe_re = pbuf[number, 0]
        probe_im = pbuf[number, 1]
        place(frame.at[1, 0], probe_re * back_re + probe_im * back_im, row, col)
        place(frame.at[1, 1], probe_re * back_im - probe_im * back_re, row, col)
        return carry

    lax.fori_loop(0, 2, second, 0)
    send_rows(1)
    send_sides(0)
    send_sides(1)
    stores = [finish(0), finish(1)]
    for copy in stores:
        copy.wait()
    for number in range(COPIES):
        copy, there, _ = copies[number]
        if there is None:
            copy.wait_send()
        else:
            pl.when(there)(copy.wait_send)


def solution(mesh):
    rows, cols = mesh.shape["gy"], mesh.shape["gx"]
    tab, atab = constant_tables()

    def step(object_field, probe, positions, residual, saved_wave):
        anywhere = pl.BlockSpec(memory_space=pl.ANY)
        vmem = pltpu.VMEM
        return pl.pallas_call(
            functools.partial(kernel, rows, cols),
            name="adjoint",
            out_shape=jax.ShapeDtypeStruct((2, 2, WIN, WIN), F32),
            in_specs=[pl.BlockSpec(memory_space=pltpu.SMEM)] + [anywhere] * 6,
            out_specs=anywhere,
            scratch_shapes=[
                vmem((2, 2, WIN, WIN), F32),
                vmem((2, WIN, WIN), F32),
                vmem((2, 1024, WIN), BF16),
                vmem((2, 2, WIN, WIN), BF16),
                vmem((4, WIN, WIN), BF16),
                vmem((4, WIN, WIN), BF16),
                vmem((2, 512, 512), F32),
                vmem((3, 8, 128), F32),
                vmem((3, 3, 8, 128), F32),
                vmem((2, 2, 512, 512), F32),
                vmem((2, 2, RIM, 512), F32),
                vmem((2, 2, RIM, WIN), F32),
                vmem((2, 2, RIM, WIN), F32),
                vmem((2, 2, RIM, RIM), F32),
                vmem((2, 2, WIN, RIM), F32),
                vmem((2, 2, WIN, RIM), F32),
                vmem((2, 2, 2, WIN, RIM), F32),
                vmem((512, 1024), BF16),
                vmem((1536, 512), BF16),
                vmem((512, 1536), BF16),
                vmem((1536, 512), BF16),
                vmem((1536, 512), BF16),
                vmem((512, 1536), BF16),
                vmem((512, 512), F32),
                vmem((2, WIN, 512), F32),
                vmem((2, 2, WIN, WIN), F32),
                vmem((2, WIN, WIN), BF16),
                vmem((WIN, WIN), F32),
                vmem((2, 2, WIN, WIN), F32),
                pltpu.SemaphoreType.DMA((COPIES,)),
                pltpu.SemaphoreType.DMA((COPIES,)),
                pltpu.SemaphoreType.DMA((10,)),
            ],
            compiler_params=pltpu.CompilerParams(
                collective_id=0, has_side_effects=True, vmem_limit_bytes=56 * 1024 * 1024
            ),
        )(
            positions.reshape(2, 2),
            object_field,
            probe,
            residual.reshape(2, 512, WIN),
            saved_wave.reshape(2, 2, WIN, WIN),
            jnp.asarray(tab),
            jnp.asarray(atab),
        )

    placed = (
        P(None, None, "gy", "gx"),
        P(),
        P("gy", "gx", None),
        P("gy", "gx", None, None, None),
        P("gy", "gx", None, None, None),
    )
    return jax.shard_map(
        step, mesh=mesh, in_specs=placed, out_specs=P(None, None, "gy", "gx"), check_vma=False
    )
```

```python
import functools
import math

import jax
import jax.numpy as jnp
import numpy as np
from jax import lax
from jax.experimental import pallas as pl
from jax.experimental.pallas import tpu as pltpu
from jax.sharding import PartitionSpec as P

fresnel_rate = 200.0
ridge = 0.5
WIN = 256
RIM = 128
MESH = pl.DeviceIdType.MESH
F32 = jnp.float32
BF16 = jnp.bfloat16

O_RIGHT, O_LEFT = 0, 2
C_INNER, C_STRAIGHT, C_DIAGONAL, C_EDGE = 4, 5, 6, 7
H_INNER, H_STRAIGHT, H_DIAGONAL = 8, 10, 11
POS_RIGHT, POS_LEFT, POS_INNER, POS_OUTER = 12, 13, 14, 15
GRAD = 16
COPIES = GRAD + 16


def split(values):
    high = values.astype(BF16)
    return high, (values - high.astype(F32)).astype(BF16)


def constant_tables():
    index = np.arange(WIN)
    angle = (np.outer(index, index) % WIN) * (2.0 * math.pi / WIN)
    freq = ((index + WIN // 2) % WIN - WIN // 2) / WIN
    phase = fresnel_rate * freq**2
    inverse = np.exp(1j * angle) / math.sqrt(WIN)
    across = inverse @ np.diag(np.exp(1j * phase)) @ np.conj(inverse)

    def pieces(table):
        parts = [table.real, table.imag]
        high = [np.asarray(t, np.float32).astype(jnp.bfloat16) for t in parts]
        low = [(t - h.astype(np.float64)).astype(np.float32).astype(jnp.bfloat16) for t, h in zip(parts, high)]
        return np.stack(high + low)

    return pieces(inverse), pieces(across)


def dot(a, b):
    return jnp.dot(a, b, preferred_element_type=F32)


def kernel(
    rows,
    cols,
    pos_hbm,
    obj_hbm,
    probe_hbm,
    res_hbm,
    sav_hbm,
    tab_hbm,
    atab_hbm,
    out,
    pos_ref,
    obj,
    probe,
    res,
    sav,
    tab,
    atab,
    ext,
    posx,
    posall,
    frame,
    within,
    straight,
    slanted,
    edge,
    from_left,
    from_right,
    side,
    left_tab,
    right_tab,
    left_a,
    right_a,
    fields,
    pair,
    big,
    gbuf,
    pbuf,
    lsq,
    light,
    send_sem,
    recv_sem,
    load_sem,
):
    gx = lax.axis_index("gx")
    gy = lax.axis_index("gy")
    core = gy % 2
    parity = (gy // 2) % 2
    out_row = gy - 1 + 2 * core
    side_col = gx - 1 + 2 * parity
    has_left, has_right = gx > 0, gx < cols - 1
    has_outer = (out_row >= 0) & (out_row < rows)
    has_side = (side_col >= 0) & (side_col < cols)
    has_diagonal = has_outer & has_side
    lone = has_outer & jnp.logical_not(has_side)
    facing = has_outer & (((gx == 0) & (parity == 1)) | ((gx == cols - 1) & (parity == 0)))
    right = {"gx": lax.rem(gx + 1, cols)}
    left = {"gx": lax.rem(gx + cols - 1, cols)}
    inner = {"gy": gy + 1 - 2 * core}
    outer = {"gy": lax.rem(out_row + rows, rows)}
    diagonal = {"gx": lax.rem(side_col + cols, cols), "gy": lax.rem(out_row + rows, rows)}

    def cut(start, size=RIM):
        return pl.ds(pl.multiple_of(start, RIM), size)

    loads = []

    def load(source, target):
        copy = pltpu.make_async_copy(source, target, load_sem.at[len(loads)])
        copy.start()
        loads.append(copy)

    load(pos_hbm, pos_ref)
    load(res_hbm, res.at[:, 0:512])
    load(res_hbm, res.at[:, 512:1024])
    load(tab_hbm, tab)
    load(sav_hbm, sav)
    load(probe_hbm, probe)
    load(atab_hbm, atab)
    load(obj_hbm.at[1], ext.at[:, RIM : 3 * RIM, RIM : 3 * RIM])
    load(obj_hbm, obj)

    frame[...] = jnp.zeros_like(frame)

    @pl.when(gx == 0)
    def _():
        ext[:, RIM : 3 * RIM, 0:RIM] = jnp.zeros((2, WIN, RIM), F32)

    @pl.when(gx == cols - 1)
    def _():
        ext[:, RIM : 3 * RIM, 3 * RIM :] = jnp.zeros((2, WIN, RIM), F32)

    barrier = pltpu.get_barrier_semaphore()
    greeted = 1
    pl.semaphore_signal(barrier, inc=1, device_id=inner, device_id_type=MESH)
    for there, who in ((has_left, left), (has_right, right), (has_outer, outer), (has_diagonal, diagonal)):
        @pl.when(there)
        def _():
            pl.semaphore_signal(barrier, inc=1, device_id=who, device_id_type=MESH)

        greeted = greeted + there.astype(jnp.int32)
    pl.semaphore_wait(barrier, greeted)

    copies = {}

    def send(source, target, number, to, there=None, comes=None):
        copy = pltpu.make_async_remote_copy(
            src_ref=source,
            dst_ref=target,
            send_sem=send_sem.at[number],
            recv_sem=recv_sem.at[number],
            device_id=to,
            device_id_type=MESH,
        )
        comes = there if comes is None else comes
        copies[number] = (copy, there, comes)
        if there is None:
            copy.start()
        else:
            pl.when(there)(copy.start)

    def arrived(*numbers):
        for number in numbers:
            copy, _, comes = copies[number]
            if comes is None:
                copy.wait_recv()
            else:
                pl.when(comes)(copy.wait_recv)

    loads[0].wait()
    for number in range(2):
        for axis in range(2):
            value = pos_ref[number, axis].astype(F32)
            posx[1, 2 * number + axis : 2 * number + axis + 1, :] = jnp.full((1, 128), value, F32)
    posx[1, 4:8, :] = jnp.zeros((4, 128), F32)
    send(posx.at[1], posx.at[0], POS_RIGHT, right, has_right, has_left)
    send(posx.at[1], posx.at[2], POS_LEFT, left, has_left, has_right)
    near = 128 * parity
    halo = 384 * parity
    over = WIN * (1 - 2 * parity)
    below = RIM * core
    above = RIM - RIM * core
    outside = 3 * RIM * (1 - core)
    inside_row = 3 * RIM * core
    for part, start in ((0, below), (1, above)):
        tall = cut(start)
        send(obj_hbm.at[1, :, tall, RIM:], ext.at[:, cut(RIM + start), 0:RIM], O_RIGHT + part, right, has_right, has_left)
        send(obj_hbm.at[1, :, tall, 0:RIM], ext.at[:, cut(RIM + start), 3 * RIM :], O_LEFT + part, left, has_left, has_right)
    send(obj_hbm.at[1, :, cut(below), cut(near)], ext.at[:, cut(outside), cut(RIM + near)], C_STRAIGHT, outer, has_outer)
    send(
        obj_hbm.at[1, :, cut(below), cut(near)],
        ext.at[:, cut(outside), cut(RIM + near + over)],
        C_DIAGONAL,
        diagonal,
        has_diagonal,
    )
    send(
        obj_hbm.at[1, :, cut(below), cut(RIM - near)],
        ext.at[:, cut(outside), cut(WIN - near)],
        C_EDGE,
        outer,
        facing,
        lone,
    )
    send(obj_hbm.at[1, :, cut(above), :], ext.at[:, cut(inside_row), RIM : 3 * RIM], C_INNER, inner)

    row_index = lax.broadcasted_iota(jnp.int32, (WIN, WIN), 0)
    col_index = lax.broadcasted_iota(jnp.int32, (WIN, WIN), 1)

    def turn(shift):
        offset = row_index - col_index
        hit = (offset == shift) | (offset == shift - WIN)
        return jnp.where(hit, 1.0, 0.0).astype(BF16)

    def turn_columns(shift):
        offset = col_index - row_index
        hit = (offset == shift) | (offset == shift - WIN)
        return jnp.where(hit, 1.0, 0.0).astype(BF16)

    def place(target, field, row, col):
        for a in range(2):
            low = row_index >= row if a == 0 else row_index < row
            for b in range(2):
                hit = low & (col_index >= col if b == 0 else col_index < col)
                spot = (slice(a * WIN, (a + 1) * WIN), slice(b * WIN, (b + 1) * WIN))
                target[spot] = target[spot] + jnp.where(hit, field, 0.0)

    for copy in loads[1:]:
        copy.wait()

    def first(number, carry):
        row = pos_ref[number, 0]
        col = pos_ref[number, 1]
        rows_turned = turn(row)
        cols_turned = turn_columns(col)
        for half in range(2):
            cos = dot(rows_turned, tab[2 * half])
            sin = dot(rows_turned, tab[2 * half + 1])
            at = 512 * half
            left_tab[0:256, at : at + 256] = cos.astype(BF16)
            left_tab[0:256, at + 256 : at + 512] = (-sin).astype(BF16)
            left_tab[256:512, at : at + 256] = sin.astype(BF16)
            left_tab[256:512, at + 256 : at + 512] = cos.astype(BF16)
            cos = dot(tab[2 * half], cols_turned)
            sin = dot(tab[2 * half + 1], cols_turned)
            for at in (0, 512) if half == 0 else (1024,):
                right_tab[at : at + 256, 0:256] = cos.astype(BF16)
                right_tab[at : at + 256, 256:512] = sin.astype(BF16)
                right_tab[at + 256 : at + 512, 0:256] = (-sin).astype(BF16)
                right_tab[at + 256 : at + 512, 256:512] = cos.astype(BF16)
        half_way = dot(left_tab[...], res[number])
        high, low = split(half_way)
        for part in range(2):
            span = slice(256 * part, 256 * part + 256)
            for at, piece in ((0, high), (512, low), (1024, high)):
                pair[0:256, at + 256 * part : at + 256 * part + 256] = piece[span]
        field = dot(pair[0:256, :], right_tab[...])
        gbuf[number] = field
        field_re = field[:, 0:256]
        field_im = field[:, 256:512]
        wave_re = dot(dot(rows_turned, sav[number, 0]).astype(BF16), cols_turned)
        wave_im = dot(dot(rows_turned, sav[number, 1]).astype(BF16), cols_turned)
        place(frame.at[0, 0], wave_re * field_re + wave_im * field_im, row, col)
        place(frame.at[0, 1], wave_re * field_im - wave_im * field_re, row, col)
        for part in range(2):
            high, low = split(probe[part])
            high = dot(dot(rows_turned, high).astype(BF16), cols_turned)
            low = dot(dot(rows_turned, low).astype(BF16), cols_turned)
            pbuf[number, part] = high + low
        return carry

    lax.fori_loop(0, 2, first, 0)

    for half in range(2):
        real = atab[2 * half]
        imag = atab[2 * half + 1]
        for at in (0, 512) if half == 0 else (1024,):
            left_a[0:256, at : at + 256] = real
            left_a[0:256, at + 256 : at + 512] = -imag
            left_a[256:512, at : at + 256] = imag
            left_a[256:512, at + 256 : at + 512] = real
            right_a[at : at + 256, 0:256] = real
            right_a[at : at + 256, 256:512] = imag
            right_a[at + 256 : at + 512, 0:256] = -imag
            right_a[at + 256 : at + 512, 256:512] = real
    high, low = split(probe[0] * probe[0] + probe[1] * probe[1])
    lsq[0] = high
    lsq[1] = low

    def send_rows(group):
        base = GRAD + 8 * group
        send(frame.at[group, :, cut(3 * RIM * core), cut(WIN - WIN * parity, WIN)], straight.at[group], base + 1, outer, has_outer)
        send(frame.at[group, :, cut(3 * RIM * core), cut(WIN * parity, WIN)], slanted.at[group], base + 2, diagonal, has_diagonal)
        send(frame.at[group, :, cut(3 * RIM * core), cut(RIM + near)], edge.at[group], base + 3, outer, lone, facing)
        send(frame.at[group, :, cut(3 * RIM - 3 * RIM * core), :], within.at[group], base, inner)

    def send_sides(group, part):
        base = GRAD + 8 * group
        start = below if part == 0 else above
        tall = cut(RIM + start)
        if part == 1:
            arrived(base)
            for plane in range(2):
                frame[group, plane, tall, :] = frame[group, plane, tall, :] + within[group, plane]
        else:
            arrived(base + 1, base + 2, base + 3)
            for plane in range(2):
                spot = (group, plane, tall, cut(WIN * parity, WIN))
                for there, piece in ((has_outer, straight), (has_diagonal, slanted)):
                    @pl.when(there)
                    def _():
                        frame[spot] = frame[spot] + piece[group, plane]

                @pl.when(facing)
                def _():
                    spot = (group, plane, tall, cut(WIN - near))
                    frame[spot] = frame[spot] + edge[group, plane]

        side[group, part, 0] = frame[group, :, tall, 3 * RIM :]
        side[group, part, 1] = frame[group, :, tall, 0:RIM]
        send(side.at[group, part, 0], from_left.at[group, :, cut(start)], base + 4 + part, right, has_right, has_left)
        send(side.at[group, part, 1], from_right.at[group, :, cut(start)], base + 6 + part, left, has_left, has_right)

    def finish(group):
        base = GRAD + 8 * group

        @pl.when(gx == 0)
        def _():
            from_left[group] = jnp.zeros((2, WIN, RIM), F32)

        @pl.when(gx == cols - 1)
        def _():
            from_right[group] = jnp.zeros((2, WIN, RIM), F32)

        arrived(base + 4, base + 5, base + 6, base + 7)
        for part in range(2):
            for v, horizontal in ((0, from_left), (1, from_right)):
                wide = slice(v * RIM, v * RIM + RIM)
                total = (
                    frame[group, part, RIM : 3 * RIM, RIM + v * RIM : 2 * RIM + v * RIM]
                    + horizontal[group, part]
                )
                out[1 - group, part, :, wide] = obj[1 - group, part, :, wide] - total / light[:, wide]

    arrived(POS_RIGHT, POS_LEFT)
    posall[1] = posx[...]
    send(posx, posall.at[2 * core], POS_INNER, inner)
    send(posx, posall.at[2 - 2 * core], POS_OUTER, outer, has_outer)
    arrived(O_RIGHT, O_LEFT)
    rows_out, rows_in = cut(RIM + below), cut(RIM + above)
    send(ext.at[:, rows_out, cut(halo)], ext.at[:, cut(outside), cut(halo)], H_STRAIGHT, outer, has_outer)
    send(ext.at[:, rows_out, cut(halo)], ext.at[:, cut(outside), cut(halo + over)], H_DIAGONAL, diagonal, has_diagonal)
    send_rows(0)

    offset = (row_index - col_index).astype(F32)

    def lit(number, carry):
        dy = number // 3 - 1
        dx = number % 3 - 1
        inside = (gy + dy >= 0) & (gy + dy < rows) & (gx + dx >= 0) & (gx + dx < cols)
        weight = jnp.where(inside, 1.0, 0.0)
        spots = posall[number // 3, number % 3]
        total = light[...]
        for spot in range(2):
            row = spots[2 * spot : 2 * spot + 1, :] + (dy * WIN - RIM).astype(F32)
            col = spots[2 * spot + 1 : 2 * spot + 2, :] + (dx * WIN - RIM).astype(F32)
            row = jnp.concatenate([row, row], axis=1)
            col = jnp.concatenate([col, col], axis=1)
            by_rows = jnp.where(offset == row, weight, 0.0).astype(BF16)
            by_cols = jnp.where(-offset == col, 1.0, 0.0).astype(BF16)
            for part in range(2):
                total = total + dot(by_rows, dot(lsq[part], by_cols).astype(BF16))
        light[...] = total
        return carry


    arrived(O_RIGHT + 1, O_LEFT + 1)
    for v, span in ((0, slice(0, RIM)), (1, slice(3 * RIM, 4 * RIM))):
        send(ext.at[:, rows_in, span], ext.at[:, cut(inside_row), span], H_INNER + v, inner)
    send_sides(0, 1)
    arrived(C_INNER, C_STRAIGHT, C_DIAGONAL, C_EDGE, H_INNER, H_INNER + 1, H_STRAIGHT, H_DIAGONAL)

    first_row = jnp.where(gy == 0, RIM, 0)
    last_row = jnp.where(gy == rows - 1, 3 * RIM, 4 * RIM)
    first_col = jnp.where(gx == 0, RIM, 0)
    last_col = jnp.where(gx == cols - 1, 3 * RIM, 4 * RIM)

    for number in range(2):
        row = pos_ref[number, 0]
        col = pos_ref[number, 1]
        upper = row_index >= row
        leftmost = col_index >= col
        at_row = jnp.where(upper, row_index, row_index + WIN)
        at_col = jnp.where(leftmost, col_index, col_index + WIN)
        inside = (at_row >= first_row) & (at_row < last_row) & (at_col >= first_col) & (at_col < last_col)
        patch = []
        for part in range(2):
            top = jnp.where(leftmost, ext[part, 0:256, 0:256], ext[part, 0:256, 256:512])
            bottom = jnp.where(leftmost, ext[part, 256:512, 0:256], ext[part, 256:512, 256:512])
            patch.append(jnp.where(inside, jnp.where(upper, top, bottom), 0.0))
        field_re = gbuf[number, :, 0:256]
        field_im = gbuf[number, :, 256:512]
        chi = (
            patch[0] * field_re + patch[1] * field_im,
            patch[0] * field_im - patch[1] * field_re,
        )
        for part in range(2):
            high, low = split(chi[part])
            for at, piece in ((0, high), (512, low), (1024, high)):
                fields[at + 256 * part : at + 256 * part + 256, 256 * number : 256 * number + 256] = piece
    big[...] = dot(left_a[...], fields[...])
    for number in range(2):
        for part in range(2):
            high, low = split(big[256 * part : 256 * part + 256, 256 * number : 256 * number + 256])
            for at, piece in ((0, high), (512, low), (1024, high)):
                pair[256 * number : 256 * number + 256, at + 256 * part : at + 256 * part + 256] = piece
    big[...] = dot(pair[...], right_a[...])

    def second(number, carry):
        row = pos_ref[number, 0]
        col = pos_ref[number, 1]
        span = pl.ds(pl.multiple_of(number * 256, 256), 256)
        back_re = big[span, 0:256]
        back_im = big[span, 256:512]
        probe_re = pbuf[number, 0]
        probe_im = pbuf[number, 1]
        place(frame.at[1, 0], probe_re * back_re + probe_im * back_im, row, col)
        place(frame.at[1, 1], probe_re * back_im - probe_im * back_re, row, col)
        return carry

    lax.fori_loop(0, 2, second, 0)
    send_rows(1)
    send_sides(0, 0)
    light[...] = jnp.full((WIN, WIN), ridge, F32)
    arrived(POS_INNER, POS_OUTER)
    lax.fori_loop(0, 9, lit, 0)
    send_sides(1, 1)
    send_sides(1, 0)
    finish(0)
    finish(1)
    for number in range(COPIES):
        copy, there, _ = copies[number]
        if there is None:
            copy.wait_send()
        else:
            pl.when(there)(copy.wait_send)


def store(result, out_hbm, sem):
    copies = [
        pltpu.make_async_copy(result.at[k // 2, k % 2], out_hbm.at[k // 2, k % 2], sem.at[k]) for k in range(4)
    ]
    for copy in copies:
        copy.start()
    for copy in copies:
        copy.wait()


def solution(mesh):
    rows, cols = mesh.shape["gy"], mesh.shape["gx"]
    tab, atab = constant_tables()

    def step(object_field, probe, positions, residual, saved_wave):
        anywhere = pl.BlockSpec(memory_space=pltpu.HBM)
        vmem = pltpu.VMEM
        result = pl.pallas_call(
            functools.partial(kernel, rows, cols),
            name="adjoint",
            out_shape=jax.ShapeDtypeStruct((2, 2, WIN, WIN), F32),
            in_specs=[anywhere] * 7,
            out_specs=pl.BlockSpec(memory_space=pltpu.VMEM),
            scratch_shapes=[
                pltpu.SMEM((2, 2), jnp.int32),
                vmem((2, 2, WIN, WIN), F32),
                vmem((2, WIN, WIN), F32),
                vmem((2, 1024, WIN), BF16),
                vmem((2, 2, WIN, WIN), BF16),
                vmem((4, WIN, WIN), BF16),
                vmem((4, WIN, WIN), BF16),
                vmem((2, 512, 512), F32),
                vmem((3, 8, 128), F32),
                vmem((3, 3, 8, 128), F32),
                vmem((2, 2, 512, 512), F32),
                vmem((2, 2, RIM, 512), F32),
                vmem((2, 2, RIM, WIN), F32),
                vmem((2, 2, RIM, WIN), F32),
                vmem((2, 2, RIM, RIM), F32),
                vmem((2, 2, WIN, RIM), F32),
                vmem((2, 2, WIN, RIM), F32),
                vmem((2, 2, 2, 2, RIM, RIM), F32),
                vmem((512, 1024), BF16),
                vmem((1536, 512), BF16),
                vmem((512, 1536), BF16),
                vmem((1536, 512), BF16),
                vmem((1536, 512), BF16),
                vmem((512, 1536), BF16),
                vmem((512, 512), F32),
                vmem((2, WIN, 512), F32),
                vmem((2, 2, WIN, WIN), F32),
                vmem((2, WIN, WIN), BF16),
                vmem((WIN, WIN), F32),
                pltpu.SemaphoreType.DMA((COPIES,)),
                pltpu.SemaphoreType.DMA((COPIES,)),
                pltpu.SemaphoreType.DMA((9,)),
            ],
            compiler_params=pltpu.CompilerParams(
                collective_id=0, has_side_effects=True, vmem_limit_bytes=40 * 1024 * 1024
            ),
        )(
            *(
                pltpu.with_memory_space_constraint(x, pltpu.HBM)
                for x in (
                    positions.reshape(2, 2),
                    object_field,
                    probe,
                    residual.reshape(2, 512, WIN),
                    saved_wave.reshape(2, 2, WIN, WIN),
                    jnp.asarray(tab),
                    jnp.asarray(atab),
                )
            ),
        )
        return pl.pallas_call(
            store,
            name="store",
            out_shape=jax.ShapeDtypeStruct((2, 2, WIN, WIN), F32),
            in_specs=[pl.BlockSpec(memory_space=pltpu.VMEM)],
            out_specs=anywhere,
            scratch_shapes=[pltpu.SemaphoreType.DMA((4,))],
            compiler_params=pltpu.CompilerParams(vmem_limit_bytes=2 * 1024 * 1024),
        )(result)

    placed = (
        P(None, None, "gy", "gx"),
        P(),
        P("gy", "gx", None),
        P("gy", "gx", None, None, None),
        P("gy", "gx", None, None, None),
    )
    return jax.shard_map(
        step, mesh=mesh, in_specs=placed, out_specs=P(None, None, "gy", "gx"), check_vma=False
    )
```

```python
import functools
import math

import jax
import jax.numpy as jnp
import numpy as np
from jax import lax
from jax.experimental import pallas as pl
from jax.experimental.pallas import tpu as pltpu
from jax.sharding import PartitionSpec as P

fresnel_rate = 200.0
ridge = 0.5
WIN = 256
RIM = 128
MESH = pl.DeviceIdType.MESH
F32 = jnp.float32
BF16 = jnp.bfloat16

O_RIGHT, O_LEFT = 0, 2
C_INNER, C_STRAIGHT, C_DIAGONAL, C_EDGE = 4, 5, 6, 7
H_INNER, H_STRAIGHT, H_DIAGONAL = 8, 10, 11
POS_RIGHT, POS_LEFT, POS_INNER, POS_OUTER = 12, 13, 14, 15
GRAD = 16
COPIES = GRAD + 16


def split(values):
    high = values.astype(BF16)
    return high, (values - high.astype(F32)).astype(BF16)


def constant_tables():
    index = np.arange(WIN)
    angle = (np.outer(index, index) % WIN) * (2.0 * math.pi / WIN)
    freq = ((index + WIN // 2) % WIN - WIN // 2) / WIN
    phase = fresnel_rate * freq**2
    inverse = np.exp(1j * angle) / math.sqrt(WIN)
    across = inverse @ np.diag(np.exp(1j * phase)) @ np.conj(inverse)

    def pieces(table):
        parts = [table.real, table.imag]
        high = [np.asarray(t, np.float32).astype(jnp.bfloat16) for t in parts]
        low = [(t - h.astype(np.float64)).astype(np.float32).astype(jnp.bfloat16) for t, h in zip(parts, high)]
        return np.stack(high + low)

    return pieces(inverse), pieces(across)


def dot(a, b):
    return jnp.dot(a, b, preferred_element_type=F32)


def kernel(
    rows,
    cols,
    pos_hbm,
    obj_hbm,
    probe_hbm,
    res_hbm,
    sav_hbm,
    tab_hbm,
    atab_hbm,
    out,
    pos_ref,
    obj,
    probe,
    res,
    sav,
    tab,
    atab,
    ext,
    posx,
    posall,
    frame,
    within,
    straight,
    slanted,
    edge,
    from_left,
    from_right,
    side,
    left_tab,
    right_tab,
    left_a,
    right_a,
    fields,
    pair,
    big,
    gbuf,
    pbuf,
    lsq,
    light,
    send_sem,
    recv_sem,
    load_sem,
):
    gx = lax.axis_index("gx")
    gy = lax.axis_index("gy")
    core = gy % 2
    parity = (gy // 2) % 2
    out_row = gy - 1 + 2 * core
    side_col = gx - 1 + 2 * parity
    has_left, has_right = gx > 0, gx < cols - 1
    has_outer = (out_row >= 0) & (out_row < rows)
    has_side = (side_col >= 0) & (side_col < cols)
    has_diagonal = has_outer & has_side
    lone = has_outer & jnp.logical_not(has_side)
    facing = has_outer & (((gx == 0) & (parity == 1)) | ((gx == cols - 1) & (parity == 0)))
    right = {"gx": lax.rem(gx + 1, cols)}
    left = {"gx": lax.rem(gx + cols - 1, cols)}
    inner = {"gy": gy + 1 - 2 * core}
    outer = {"gy": lax.rem(out_row + rows, rows)}
    diagonal = {"gx": lax.rem(side_col + cols, cols), "gy": lax.rem(out_row + rows, rows)}

    def cut(start, size=RIM):
        return pl.ds(pl.multiple_of(start, RIM), size)

    barrier = pltpu.get_barrier_semaphore()
    greeted = 1
    pl.semaphore_signal(barrier, inc=1, device_id=inner, device_id_type=MESH)
    for there, who in ((has_left, left), (has_right, right), (has_outer, outer), (has_diagonal, diagonal)):
        @pl.when(there)
        def _():
            pl.semaphore_signal(barrier, inc=1, device_id=who, device_id_type=MESH)

        greeted = greeted + there.astype(jnp.int32)
    loads = []

    def load(source, target):
        copy = pltpu.make_async_copy(source, target, load_sem.at[len(loads)])
        copy.start()
        loads.append(copy)

    load(pos_hbm, pos_ref)
    load(res_hbm, res.at[:, 0:512])
    load(res_hbm, res.at[:, 512:1024])
    load(tab_hbm, tab)
    load(sav_hbm, sav)
    load(probe_hbm, probe)
    load(atab_hbm, atab)
    load(obj_hbm.at[1], ext.at[:, RIM : 3 * RIM, RIM : 3 * RIM])
    load(obj_hbm, obj)

    frame[...] = jnp.zeros_like(frame)

    @pl.when(gx == 0)
    def _():
        ext[:, RIM : 3 * RIM, 0:RIM] = jnp.zeros((2, WIN, RIM), F32)

    @pl.when(gx == cols - 1)
    def _():
        ext[:, RIM : 3 * RIM, 3 * RIM :] = jnp.zeros((2, WIN, RIM), F32)

    pl.semaphore_wait(barrier, greeted)

    copies = {}

    def send(source, target, number, to, there=None, comes=None):
        copy = pltpu.make_async_remote_copy(
            src_ref=source,
            dst_ref=target,
            send_sem=send_sem.at[number],
            recv_sem=recv_sem.at[number],
            device_id=to,
            device_id_type=MESH,
        )
        comes = there if comes is None else comes
        copies[number] = (copy, there, comes)
        if there is None:
            copy.start()
        else:
            pl.when(there)(copy.start)

    def arrived(*numbers):
        for number in numbers:
            copy, _, comes = copies[number]
            if comes is None:
                copy.wait_recv()
            else:
                pl.when(comes)(copy.wait_recv)

    loads[0].wait()
    for number in range(2):
        for axis in range(2):
            value = pos_ref[number, axis].astype(F32)
            posx[1, 2 * number + axis : 2 * number + axis + 1, :] = jnp.full((1, 128), value, F32)
    posx[1, 4:8, :] = jnp.zeros((4, 128), F32)
    send(posx.at[1], posx.at[0], POS_RIGHT, right, has_right, has_left)
    send(posx.at[1], posx.at[2], POS_LEFT, left, has_left, has_right)
    near = 128 * parity
    halo = 384 * parity
    over = WIN * (1 - 2 * parity)
    below = RIM * core
    above = RIM - RIM * core
    outside = 3 * RIM * (1 - core)
    inside_row = 3 * RIM * core
    for part, start in ((0, below), (1, above)):
        tall = cut(start)
        send(obj_hbm.at[1, :, tall, RIM:], ext.at[:, cut(RIM + start), 0:RIM], O_RIGHT + part, right, has_right, has_left)
        send(obj_hbm.at[1, :, tall, 0:RIM], ext.at[:, cut(RIM + start), 3 * RIM :], O_LEFT + part, left, has_left, has_right)
    send(obj_hbm.at[1, :, cut(below), cut(near)], ext.at[:, cut(outside), cut(RIM + near)], C_STRAIGHT, outer, has_outer)
    send(
        obj_hbm.at[1, :, cut(below), cut(near)],
        ext.at[:, cut(outside), cut(RIM + near + over)],
        C_DIAGONAL,
        diagonal,
        has_diagonal,
    )
    send(
        obj_hbm.at[1, :, cut(below), cut(RIM - near)],
        ext.at[:, cut(outside), cut(WIN - near)],
        C_EDGE,
        outer,
        facing,
        lone,
    )
    send(obj_hbm.at[1, :, cut(above), :], ext.at[:, cut(inside_row), RIM : 3 * RIM], C_INNER, inner)

    row_index = lax.broadcasted_iota(jnp.int32, (WIN, WIN), 0)
    col_index = lax.broadcasted_iota(jnp.int32, (WIN, WIN), 1)

    def turn(shift):
        offset = row_index - col_index
        hit = (offset == shift) | (offset == shift - WIN)
        return jnp.where(hit, 1.0, 0.0).astype(BF16)

    def turn_columns(shift):
        offset = col_index - row_index
        hit = (offset == shift) | (offset == shift - WIN)
        return jnp.where(hit, 1.0, 0.0).astype(BF16)

    def place(target, field, row, col):
        for a in range(2):
            low = row_index >= row if a == 0 else row_index < row
            for b in range(2):
                hit = low & (col_index >= col if b == 0 else col_index < col)
                spot = (slice(a * WIN, (a + 1) * WIN), slice(b * WIN, (b + 1) * WIN))
                target[spot] = target[spot] + jnp.where(hit, field, 0.0)

    for copy in loads[1:]:
        copy.wait()

    def first(number, carry):
        row = pos_ref[number, 0]
        col = pos_ref[number, 1]
        rows_turned = turn(row)
        cols_turned = turn_columns(col)
        for half in range(2):
            cos = dot(rows_turned, tab[2 * half])
            sin = dot(rows_turned, tab[2 * half + 1])
            at = 512 * half
            left_tab[0:256, at : at + 256] = cos.astype(BF16)
            left_tab[0:256, at + 256 : at + 512] = (-sin).astype(BF16)
            left_tab[256:512, at : at + 256] = sin.astype(BF16)
            left_tab[256:512, at + 256 : at + 512] = cos.astype(BF16)
            cos = dot(tab[2 * half], cols_turned)
            sin = dot(tab[2 * half + 1], cols_turned)
            for at in (0, 512) if half == 0 else (1024,):
                right_tab[at : at + 256, 0:256] = cos.astype(BF16)
                right_tab[at : at + 256, 256:512] = sin.astype(BF16)
                right_tab[at + 256 : at + 512, 0:256] = (-sin).astype(BF16)
                right_tab[at + 256 : at + 512, 256:512] = cos.astype(BF16)
        half_way = dot(left_tab[...], res[number])
        high, low = split(half_way)
        for part in range(2):
            span = slice(256 * part, 256 * part + 256)
            for at, piece in ((0, high), (512, low), (1024, high)):
                pair[0:256, at + 256 * part : at + 256 * part + 256] = piece[span]
        field = dot(pair[0:256, :], right_tab[...])
        gbuf[number] = field
        field_re = field[:, 0:256]
        field_im = field[:, 256:512]
        wave_re = dot(dot(rows_turned, sav[number, 0]).astype(BF16), cols_turned)
        wave_im = dot(dot(rows_turned, sav[number, 1]).astype(BF16), cols_turned)
        place(frame.at[0, 0], wave_re * field_re + wave_im * field_im, row, col)
        place(frame.at[0, 1], wave_re * field_im - wave_im * field_re, row, col)
        for part in range(2):
            high, low = split(probe[part])
            high = dot(dot(rows_turned, high).astype(BF16), cols_turned)
            low = dot(dot(rows_turned, low).astype(BF16), cols_turned)
            pbuf[number, part] = high + low
        return carry

    lax.fori_loop(0, 2, first, 0)

    for half in range(2):
        real = atab[2 * half]
        imag = atab[2 * half + 1]
        for at in (0, 512) if half == 0 else (1024,):
            left_a[0:256, at : at + 256] = real
            left_a[0:256, at + 256 : at + 512] = -imag
            left_a[256:512, at : at + 256] = imag
            left_a[256:512, at + 256 : at + 512] = real
            right_a[at : at + 256, 0:256] = real
            right_a[at : at + 256, 256:512] = imag
            right_a[at + 256 : at + 512, 0:256] = -imag
            right_a[at + 256 : at + 512, 256:512] = real
    high, low = split(probe[0] * probe[0] + probe[1] * probe[1])
    lsq[0] = high
    lsq[1] = low

    def send_rows(group):
        base = GRAD + 8 * group
        send(frame.at[group, :, cut(3 * RIM * core), cut(WIN - WIN * parity, WIN)], straight.at[group], base + 1, outer, has_outer)
        send(frame.at[group, :, cut(3 * RIM * core), cut(WIN * parity, WIN)], slanted.at[group], base + 2, diagonal, has_diagonal)
        send(frame.at[group, :, cut(3 * RIM * core), cut(RIM + near)], edge.at[group], base + 3, outer, lone, facing)
        send(frame.at[group, :, cut(3 * RIM - 3 * RIM * core), :], within.at[group], base, inner)

    def send_sides(group, part):
        base = GRAD + 8 * group
        start = below if part == 0 else above
        tall = cut(RIM + start)
        if part == 1:
            arrived(base)
            for plane in range(2):
                frame[group, plane, tall, :] = frame[group, plane, tall, :] + within[group, plane]
        else:
            arrived(base + 1, base + 2, base + 3)
            for plane in range(2):
                spot = (group, plane, tall, cut(WIN * parity, WIN))
                for there, piece in ((has_outer, straight), (has_diagonal, slanted)):
                    @pl.when(there)
                    def _():
                        frame[spot] = frame[spot] + piece[group, plane]

                @pl.when(facing)
                def _():
                    spot = (group, plane, tall, cut(WIN - near))
                    frame[spot] = frame[spot] + edge[group, plane]

        side[group, part, 0] = frame[group, :, tall, 3 * RIM :]
        side[group, part, 1] = frame[group, :, tall, 0:RIM]
        send(side.at[group, part, 0], from_left.at[group, :, cut(start)], base + 4 + part, right, has_right, has_left)
        send(side.at[group, part, 1], from_right.at[group, :, cut(start)], base + 6 + part, left, has_left, has_right)

    def finish(group):
        base = GRAD + 8 * group

        @pl.when(gx == 0)
        def _():
            from_left[group] = jnp.zeros((2, WIN, RIM), F32)

        @pl.when(gx == cols - 1)
        def _():
            from_right[group] = jnp.zeros((2, WIN, RIM), F32)

        arrived(base + 4, base + 5, base + 6, base + 7)
        for part in range(2):
            for v, horizontal in ((0, from_left), (1, from_right)):
                wide = slice(v * RIM, v * RIM + RIM)
                total = (
                    frame[group, part, RIM : 3 * RIM, RIM + v * RIM : 2 * RIM + v * RIM]
                    + horizontal[group, part]
                )
                out[1 - group, part, :, wide] = obj[1 - group, part, :, wide] - total / light[:, wide]

    offset = (row_index - col_index).astype(F32)

    def lit(line, dx_index, carry):
        dy = line - 1
        dx = dx_index - 1
        inside = (gy + dy >= 0) & (gy + dy < rows) & (gx + dx >= 0) & (gx + dx < cols)
        weight = jnp.where(inside, 1.0, 0.0)
        spots = posall[line, dx_index]
        total = light[...]
        for spot in range(2):
            row = spots[2 * spot : 2 * spot + 1, :] + jnp.asarray(dy * WIN - RIM, jnp.int32).astype(F32)
            col = spots[2 * spot + 1 : 2 * spot + 2, :] + (dx * WIN - RIM).astype(F32)
            row = jnp.concatenate([row, row], axis=1)
            col = jnp.concatenate([col, col], axis=1)
            by_rows = jnp.where(offset == row, weight, 0.0).astype(BF16)
            by_cols = jnp.where(-offset == col, 1.0, 0.0).astype(BF16)
            for part in range(2):
                total = total + dot(by_rows, dot(lsq[part], by_cols).astype(BF16))
        light[...] = total
        return carry

    def light_of(line):
        lax.fori_loop(0, 3, functools.partial(lit, line), 0)

    arrived(POS_RIGHT, POS_LEFT)
    posall[1] = posx[...]
    send(posx, posall.at[2 * core], POS_INNER, inner)
    send(posx, posall.at[2 - 2 * core], POS_OUTER, outer, has_outer)
    light[...] = jnp.full((WIN, WIN), ridge, F32)
    light_of(1)
    arrived(O_RIGHT, O_LEFT)
    rows_out, rows_in = cut(RIM + below), cut(RIM + above)
    send(ext.at[:, rows_out, cut(halo)], ext.at[:, cut(outside), cut(halo)], H_STRAIGHT, outer, has_outer)
    send(ext.at[:, rows_out, cut(halo)], ext.at[:, cut(outside), cut(halo + over)], H_DIAGONAL, diagonal, has_diagonal)
    send_rows(0)


    arrived(O_RIGHT + 1, O_LEFT + 1)
    for v, span in ((0, slice(0, RIM)), (1, slice(3 * RIM, 4 * RIM))):
        send(ext.at[:, rows_in, span], ext.at[:, cut(inside_row), span], H_INNER + v, inner)
    send_sides(0, 1)
    arrived(C_INNER, C_STRAIGHT, C_DIAGONAL, C_EDGE, H_INNER, H_INNER + 1, H_STRAIGHT, H_DIAGONAL)

    first_row = jnp.where(gy == 0, RIM, 0)
    last_row = jnp.where(gy == rows - 1, 3 * RIM, 4 * RIM)
    first_col = jnp.where(gx == 0, RIM, 0)
    last_col = jnp.where(gx == cols - 1, 3 * RIM, 4 * RIM)

    for number in range(2):
        row = pos_ref[number, 0]
        col = pos_ref[number, 1]
        upper = row_index >= row
        leftmost = col_index >= col
        at_row = jnp.where(upper, row_index, row_index + WIN)
        at_col = jnp.where(leftmost, col_index, col_index + WIN)
        inside = (at_row >= first_row) & (at_row < last_row) & (at_col >= first_col) & (at_col < last_col)
        patch = []
        for part in range(2):
            top = jnp.where(leftmost, ext[part, 0:256, 0:256], ext[part, 0:256, 256:512])
            bottom = jnp.where(leftmost, ext[part, 256:512, 0:256], ext[part, 256:512, 256:512])
            patch.append(jnp.where(inside, jnp.where(upper, top, bottom), 0.0))
        field_re = gbuf[number, :, 0:256]
        field_im = gbuf[number, :, 256:512]
        chi = (
            patch[0] * field_re + patch[1] * field_im,
            patch[0] * field_im - patch[1] * field_re,
        )
        for part in range(2):
            high, low = split(chi[part])
            for at, piece in ((0, high), (512, low), (1024, high)):
                fields[at + 256 * part : at + 256 * part + 256, 256 * number : 256 * number + 256] = piece
    big[...] = dot(left_a[...], fields[...])
    for number in range(2):
        for part in range(2):
            high, low = split(big[256 * part : 256 * part + 256, 256 * number : 256 * number + 256])
            for at, piece in ((0, high), (512, low), (1024, high)):
                pair[256 * number : 256 * number + 256, at + 256 * part : at + 256 * part + 256] = piece
    big[...] = dot(pair[...], right_a[...])

    def second(number, carry):
        row = pos_ref[number, 0]
        col = pos_ref[number, 1]
        span = pl.ds(pl.multiple_of(number * 256, 256), 256)
        back_re = big[span, 0:256]
        back_im = big[span, 256:512]
        probe_re = pbuf[number, 0]
        probe_im = pbuf[number, 1]
        place(frame.at[1, 0], probe_re * back_re + probe_im * back_im, row, col)
        place(frame.at[1, 1], probe_re * back_im - probe_im * back_re, row, col)
        return carry

    lax.fori_loop(0, 2, second, 0)
    send_rows(1)
    send_sides(1, 1)
    send_sides(0, 0)
    arrived(POS_INNER)
    light_of(2 - 2 * core)
    send_sides(1, 0)
    arrived(POS_OUTER)
    light_of(2 * core)
    finish(0)
    finish(1)
    for number in range(COPIES):
        copy, there, _ = copies[number]
        if there is None:
            copy.wait_send()
        else:
            pl.when(there)(copy.wait_send)


def store(result, out_hbm, sem):
    copies = [
        pltpu.make_async_copy(result.at[k // 2, k % 2], out_hbm.at[k // 2, k % 2], sem.at[k]) for k in range(4)
    ]
    for copy in copies:
        copy.start()
    for copy in copies:
        copy.wait()


def solution(mesh):
    rows, cols = mesh.shape["gy"], mesh.shape["gx"]
    tab, atab = constant_tables()

    def step(object_field, probe, positions, residual, saved_wave):
        anywhere = pl.BlockSpec(memory_space=pltpu.HBM)
        vmem = pltpu.VMEM
        result = pl.pallas_call(
            functools.partial(kernel, rows, cols),
            name="adjoint",
            out_shape=jax.ShapeDtypeStruct((2, 2, WIN, WIN), F32),
            in_specs=[anywhere] * 7,
            out_specs=pl.BlockSpec(memory_space=pltpu.VMEM),
            scratch_shapes=[
                pltpu.SMEM((2, 2), jnp.int32),
                vmem((2, 2, WIN, WIN), F32),
                vmem((2, WIN, WIN), F32),
                vmem((2, 1024, WIN), BF16),
                vmem((2, 2, WIN, WIN), BF16),
                vmem((4, WIN, WIN), BF16),
                vmem((4, WIN, WIN), BF16),
                vmem((2, 512, 512), F32),
                vmem((3, 8, 128), F32),
                vmem((3, 3, 8, 128), F32),
                vmem((2, 2, 512, 512), F32),
                vmem((2, 2, RIM, 512), F32),
                vmem((2, 2, RIM, WIN), F32),
                vmem((2, 2, RIM, WIN), F32),
                vmem((2, 2, RIM, RIM), F32),
                vmem((2, 2, WIN, RIM), F32),
                vmem((2, 2, WIN, RIM), F32),
                vmem((2, 2, 2, 2, RIM, RIM), F32),
                vmem((512, 1024), BF16),
                vmem((1536, 512), BF16),
                vmem((512, 1536), BF16),
                vmem((1536, 512), BF16),
                vmem((1536, 512), BF16),
                vmem((512, 1536), BF16),
                vmem((512, 512), F32),
                vmem((2, WIN, 512), F32),
                vmem((2, 2, WIN, WIN), F32),
                vmem((2, WIN, WIN), BF16),
                vmem((WIN, WIN), F32),
                pltpu.SemaphoreType.DMA((COPIES,)),
                pltpu.SemaphoreType.DMA((COPIES,)),
                pltpu.SemaphoreType.DMA((9,)),
            ],
            compiler_params=pltpu.CompilerParams(
                collective_id=0, has_side_effects=True, vmem_limit_bytes=40 * 1024 * 1024
            ),
        )(
            *(
                pltpu.with_memory_space_constraint(x, pltpu.HBM)
                for x in (
                    positions.reshape(2, 2),
                    object_field,
                    probe,
                    residual.reshape(2, 512, WIN),
                    saved_wave.reshape(2, 2, WIN, WIN),
                    jnp.asarray(tab),
                    jnp.asarray(atab),
                )
            ),
        )
        return pl.pallas_call(
            store,
            name="store",
            out_shape=jax.ShapeDtypeStruct((2, 2, WIN, WIN), F32),
            in_specs=[pl.BlockSpec(memory_space=pltpu.VMEM)],
            out_specs=anywhere,
            scratch_shapes=[pltpu.SemaphoreType.DMA((4,))],
            compiler_params=pltpu.CompilerParams(vmem_limit_bytes=2 * 1024 * 1024),
        )(result)

    placed = (
        P(None, None, "gy", "gx"),
        P(),
        P("gy", "gx", None),
        P("gy", "gx", None, None, None),
        P("gy", "gx", None, None, None),
    )
    return jax.shard_map(
        step, mesh=mesh, in_specs=placed, out_specs=P(None, None, "gy", "gx"), check_vma=False
    )
```
